32 devices in a mesh: member: 1, tile: 32 (over z, y, x, core).
Axes of the slice: x: 2, y: 2, z: 4, core: 2. Of those that a mesh axis runs over, the one named last changes fastest.
Arguments:
- forcing: bfloat16 [128, 8, 10, 128], P(('member', 'tile')), may hold values from -6 to 6
- ice_state: bfloat16 [1024, 128, 128], P(('member', 'tile')), may hold values from -6 to 6
- sensitivity: bfloat16 [1024, 128, 128], P(('member', 'tile')), may hold values from -6 to 6
- owner_device: int32 [1024, 4], P('tile'), may hold values from 0 to 31, all different within a row; in each aligned block of 32 rows (0 to 31, 32 to 63, ...) at most 8 rows name the same one
- panel_slot: int32 [1024, 4], P('tile'), may hold values from 0 to 3
- row_offset: int32 [1024, 4], P('tile'), may hold values from 0 to 7
- intersection_weight: float32 [1024, 4], P('tile'), may hold values from 0.2 to 1
- col_map: float32 [128, 128], replicated, may hold values from 0 to 1
- ocean_mask: int32 [1024, 128], P('tile'), may hold values 0 or 1
- lift_weight: bfloat16 [10, 128], replicated, may hold values from -1 to 1
- conv_weight: bfloat16 [3, 3, 3, 128, 128], replicated, may hold values from -0.1875 to 0.1875
- conv_bias: float32 [3, 128], replicated, may hold values from -3 to 3
Outputs:
- imitated: bfloat16 [1024, 128, 128], P(('member', 'tile'))
- state_grad: bfloat16 [1024, 128, 128], P(('member', 'tile'))
- forcing_grad: float32 [128, 8, 10, 128], P(('member', 'tile'))
The draws below stay inside these ranges and needn't reach their ends.
Inputs may be any that keep to these rules, and one draw needn't show every extreme that they name: `owner_device`: each ice row names 4 different owners; in the rows of one device no owner is named by more than 8 intersections, and that count is reached.
All inputs are finite; a program needn't handle non-finite values. No bound on the sum of `ocean_mask` on one device may be relied on, other than what follows from the above.
Results may differ from the reference program's by a relative error of at most 0.015.
Values may be sent and summed in bfloat16 or wider, within the bound.
A program may use at most 128 MiB of HBM per device.

```python
import math
import jax
import jax.numpy as jnp
import numpy as np
from jax import lax

C = 128
F = 10
L = 3
K = 4
PC = 128
COLS = 128
ROWS_DEV = 32
PR = 8
PAN_DEV = 4
ROWS = 1024
NPAN = 128
OWNERS = 32
CAP = 8


def draw_col_map(key, part):
    row_pos = jnp.arange(PC, dtype=jnp.int32)[:, None]
    col_pos = jnp.arange(COLS, dtype=jnp.int32)[None, :]
    centre = col_pos * PC // COLS
    inside = jnp.abs(row_pos - centre) <= 1
    values = jax.random.uniform(key, (PC, COLS), jnp.float32, 0.2, 1.0)
    return jnp.where(inside, values, jnp.float32(0.0)).astype(jnp.float32)


def place_ends(result, stream_key, smallest, high):
    shape = result.shape
    place = [jax.random.randint(jax.random.fold_in(stream_key, axis), (), 0, shape[axis]) for axis in range(len(shape))]
    result = result.at[tuple(place)].set(smallest)
    longest = shape.index(max(shape))
    place[longest] = (place[longest] + 1) % shape[longest]
    return result.at[tuple(place)].set(high)


def shard_levels(own_key, dims, pieces, low, top_value):
    level, own = 1.0, jax.random.fold_in(own_key, 6)
    for dim, shards_of in pieces:
        steps = jnp.exp(jax.random.uniform(jax.random.fold_in(own, dim), (shards_of,), jnp.float32, low / len(pieces), top_value / len(pieces)))
        level = level * jnp.repeat(steps, dims[dim] // shards_of).reshape([-1 if axis == dim else 1 for axis in range(len(dims))])
    return level


def assign_block(stream_key, own, number, rows, count, top, limit, slope):
    order = jax.random.permutation(stream_key, count)
    heavy_load, common = load_shares(count, rows * top, limit, slope, True), load_shares(count, rows * top, limit, slope, False)
    places = jnp.arange(count)

    def named(sizes, offset_by):
        used = int((sizes > 0).sum())
        fixed = max(1, used // 4)
        passed = fixed + (places - fixed + offset_by * (used - fixed)) % max(1, count - fixed)
        return jnp.zeros((count,), jnp.int32).at[order[jnp.where(places < fixed, places, passed)]].set(jnp.asarray(sizes, jnp.int32))

    sizes = jnp.where(number % 4 == 0, named(heavy_load, number // 4), named(common, number - number // 4 - 1))
    mixed = jax.random.permutation(jax.random.fold_in(own, 3), count)
    giver, taker = mixed[0:count // 2 * 2:2], mixed[1:count // 2 * 2:2]
    margin = jnp.minimum(sizes[giver] - 1, limit - sizes[taker]) // 2
    margin = jnp.where((giver == order[0]) | (taker == order[0]) | (sizes[taker] == 0), 0, jnp.maximum(margin, 0))
    passed = jax.random.randint(jax.random.fold_in(own, 4), (count // 2,), 0, 1 << 20) % (margin + 1)
    sizes = sizes.at[giver].add(-passed).at[taker].add(passed)
    items = jnp.searchsorted(jnp.cumsum(sizes), jnp.arange(rows * top), side="right").astype(jnp.int32)
    grid = items.reshape(top, rows).T
    grid = grid[jax.random.permutation(jax.random.fold_in(own, 1), rows)]
    offset_by = jax.random.randint(jax.random.fold_in(own, 2), (rows, 1), 0, top)
    return jnp.take_along_axis(grid, (jnp.arange(top)[None, :] + offset_by) % top, axis=1)


def load_shares(count, total, reach, lean, full):
    portions = [(1 << 20) // math.isqrt(rank ** lean) + 1 for rank in range(1, count + 1)]
    largest = reach if full else min(reach, max(-(-total // count), total * portions[0] // sum(portions)))
    least = 1 if total - largest >= count - 1 else 0
    given, surplus = [largest] + [least] * (count - 1), total - largest - least * (count - 1)
    while surplus > 0:
        free = [i for i in range(1, count) if given[i] < largest] or [i for i in range(1, count) if given[i] < reach]
        mass, left = sum([portions[i] for i in free]), surplus
        for i in free:
            addition = min(reach - given[i], max(1, left * portions[i] // mass), surplus)
            given[i] = given[i] + addition
            surplus = surplus - addition
    return np.array(given)


def scatter_about(own_key, shape, deviation, limit, cuts=(), kind=jnp.bfloat16):
    array = jax.random.normal(own_key, shape, jnp.float32) * deviation
    if len(cuts) > 0:
        array = shard_levels(own_key, shape, cuts, -0.22, 0.18) * array
    return jnp.clip(array, min=-limit, max=limit).astype(kind)


def setup_inputs(seed: int = 0, part: int = 0) -> dict:
    key_of = jax.random.split(jax.random.key(seed), 13)
    own_keys = jax.random.split(jax.random.fold_in(key_of[12], part), 13)
    forcing = scatter_about(own_keys[0], (NPAN, PR, F, PC), 1.0, 6.0, ((0, 32),))
    ice_state = scatter_about(own_keys[1], (ROWS, COLS, C), 1.0, 6.0, ((0, 32),))
    sensitivity = scatter_about(own_keys[2], (ROWS, COLS, C), 1.0, 6.0, ((0, 32),))
    owner_device_keys = jax.random.split(jax.random.fold_in(key_of[3], 1), ROWS // ROWS_DEV)
    owner_device_turns = jax.random.permutation(jax.random.fold_in(key_of[3], 3), ROWS // ROWS_DEV)
    owner_device = jax.vmap(lambda own, number: assign_block(jax.random.fold_in(key_of[3], 2), own, number, ROWS_DEV, OWNERS, K, CAP, 2))(owner_device_keys, owner_device_turns).reshape((ROWS, K))
    panel_slot = place_ends(jax.random.randint(key_of[4], (ROWS, K), 0, PAN_DEV), jax.random.fold_in(key_of[4], 1), 0, PAN_DEV - 1).astype(jnp.int32)
    row_offset = place_ends(jax.random.randint(key_of[5], (ROWS, K), 0, PR), jax.random.fold_in(key_of[5], 1), 0, PR - 1).astype(jnp.int32)
    intersection_weight = jnp.clip(jnp.exp(math.log(1.0) - 1.609438 * jax.random.uniform(key_of[6], (ROWS, K), jnp.float32) ** shard_levels(key_of[6], (ROWS, K), ((0, 32),), -0.2, 0.2)), 0.2, 1.0)
    col_map = draw_col_map(jax.random.fold_in(key_of[12], 71), part)
    ocean_mask = place_ends((jax.random.randint(key_of[8], (ROWS, COLS), 0, 4) < 3).astype(jnp.int32), jax.random.fold_in(key_of[8], 1), 0, 1)
    lift_weight = scatter_about(key_of[9], (F, C), (4 * F) ** -0.5, 1.0)
    conv_weight = scatter_about(key_of[10], (L, 3, 3, C, C), (9 * C) ** -0.5, 0.1875)
    conv_bias = scatter_about(key_of[11], (L, C), 0.5, 3.0, (), jnp.float32)
    return {"forcing": forcing, "ice_state": ice_state, "sensitivity": sensitivity, "owner_device": owner_device, "panel_slot": panel_slot, "row_offset": row_offset, "intersection_weight": intersection_weight, "col_map": col_map, "ocean_mask": ocean_mask, "lift_weight": lift_weight, "conv_weight": conv_weight, "conv_bias": conv_bias}


def convolve(field, kernel):
    return lax.conv_general_dilated(field[None].astype(jnp.float32), kernel.astype(jnp.float32), (1, 1), ((1, 1), (1, 1)), dimension_numbers=("NHWC", "HWIO", "NHWC"), precision=lax.Precision.HIGHEST)[0]


def reference(forcing, ice_state, sensitivity, owner_device, panel_slot, row_offset, intersection_weight, col_map, ocean_mask, lift_weight, conv_weight, conv_bias):
    highest = lax.Precision.HIGHEST
    flat_panels = forcing.reshape(NPAN * PR, F, PC)
    global_row = ((owner_device * PAN_DEV + panel_slot) * PR + row_offset).astype(jnp.int32)
    picked = flat_panels[global_row].astype(jnp.float32)
    mapped = jnp.einsum("rkfp,pc->rkfc", picked, col_map, precision=highest)
    ice_forcing = jnp.sum(intersection_weight[:, :, None, None] * mapped, axis=1).astype(jnp.bfloat16)
    lifted = jnp.einsum("rfc,fh->rch", ice_forcing.astype(jnp.float32), lift_weight.astype(jnp.float32), precision=highest)
    ocean_cells = ocean_mask.astype(jnp.float32)[:, :, None]
    hidden = ice_state
    tangents = []
    for layer_index in range(L):
        if layer_index == 1:
            hidden = (hidden.astype(jnp.float32) + lifted).astype(jnp.bfloat16)
        tangent = jnp.tanh(convolve(hidden, conv_weight[layer_index]) + conv_bias[layer_index])
        tangents.append(tangent)
        hidden = (hidden.astype(jnp.float32) + ocean_cells * tangent).astype(jnp.bfloat16)
    imitated = hidden
    adjoint = sensitivity.astype(jnp.float32)
    force_grad = jnp.zeros((ROWS, F, COLS), jnp.float32)
    for layer_index in reversed(range(L)):
        tangent = tangents[layer_index]
        delta_act = (adjoint * ocean_cells * (1.0 - tangent * tangent)).astype(jnp.bfloat16)
        flipped = jnp.flip(conv_weight[layer_index], (0, 1)).transpose(0, 1, 3, 2)
        adjoint = adjoint + convolve(delta_act, flipped)
        if layer_index == 1:
            force_grad = jnp.einsum("rch,fh->rfc", adjoint, lift_weight.astype(jnp.float32), precision=highest)
    projected = jnp.einsum("rfc,pc->rfp", force_grad, col_map, precision=highest)
    row_terms = intersection_weight[:, :, None, None] * projected[:, None]
    forcing_grad = jnp.zeros((NPAN * PR, F, PC), jnp.float32).at[global_row.reshape(-1)].add(row_terms.reshape(ROWS * K, F, PC))
    return imitated, adjoint.astype(jnp.bfloat16), forcing_grad.reshape(NPAN, PR, F, PC)
```

```python
import functools

import jax
import jax.numpy as jnp
from jax import lax
from jax.experimental import pallas as pl
from jax.experimental.pallas import tpu as pltpu
from jax.sharding import PartitionSpec as P

F = 10
K = 4
ROWS_DEV = 32
FP = 16
PLANE = 8
OWN = 32
WIDE = F * 128
HALF = WIDE // 2
E = 48
STEP = 4
f32, bf16 = jnp.float32, jnp.bfloat16

PLAN = (
    ('arrive', 0),
    ('lift', 0),
    ('lift', 1),
    ('conv', 1, 0, 4),
    ('arrive', 1),
    ('lift', 2),
    ('sens',),
    ('conv', 2, 0, 3),
    ('conv', 1, 4, 4),
    ('lift', 3),
    ('conv', 3, 0, 2),
    ('conv', 2, 3, 4),
    ('conv', 1, 8, 4),
    ('arrive', 2),
    ('lift', 4),
    ('conv', 4, 0, 1),
    ('conv', 3, 2, 4),
    ('conv', 2, 7, 4),
    ('conv', 1, 12, 4),
    ('lift', 5),
    ('conv', 4, 1, 4),
    ('conv', 3, 6, 4),
    ('conv', 2, 11, 4),
    ('conv', 1, 16, 4),
    ('project', 0),
    ('conv', 4, 5, 4),
    ('conv', 3, 10, 4),
    ('conv', 2, 15, 4),
    ('project', 1),
    ('conv', 4, 9, 4),
    ('conv', 3, 14, 4),
    ('project', 2),
    ('relay', 0),
    ('conv', 4, 13, 4),
    ('project', 3),
    ('relay', 1),
    ('conv', 5, 0, 4),
    ('relay', 2),
    ('conv', 5, 4, 8),
    ('relay', 3),
    ('conv', 5, 12, 4),
)


def dot(a, b, ca=1, cb=0):
    return lax.dot_general(a, b, (((ca,), (cb,)), ((), ())), preferred_element_type=f32)


def iota(shape, dim):
    return lax.broadcasted_iota(jnp.int32, shape, dim)


def remote(src, dst, send, recv, target):
    return pltpu.make_async_remote_copy(
        src_ref=src, dst_ref=dst, send_sem=send, recv_sem=recv,
        device_id={"tile": target}, device_id_type=pl.DeviceIdType.MESH,
    )


def program_kernel(
    n, ice, sens, ocean, own_t, slot_t, off_t, w_t, forc, col_map, lift, cw, cb,
    img, sg, grad,
    info_s, info, near, ext_s, ext, f2, f3, fs, wsum, ps, pv, prg, vt, ts, tr, l16, iceh, sensh, och,
    xa, xb, s0, s1, mask, g, h1, wall, oc, icr, fg, icev, sensv, cwv, bd,
    ss1, rs1, ss2, rs2, ss3, rs3, ss4, rs4, ss5, rs5, ss6, rs6, ss7, rs7, ss8, rs8, ss9, rs9, ls,
):
    me = lax.axis_index("tile")
    right, left = lax.rem(me + 1, n), lax.rem(me + n - 1, n)
    nz = n // PLANE
    z, p = lax.div(me, PLANE), lax.rem(me, PLANE)
    chip, core = lax.div(p, 2), lax.rem(p, 2)
    sibling = me + 1 - 2 * core
    mine = core * nz + z
    barrier = pltpu.get_barrier_semaphore()

    line_peers = [lax.rem(z + j, nz) * PLANE + p for j in range(1, nz)]
    plane_peers = [z * PLANE + lax.rem(chip + j, 4) * 2 + core for j in range(1, 4)]
    cross_peers = [lax.rem(z + j, nz) * PLANE + p + 1 - 2 * core for j in range(nz)]
    for peer in [left, right] + line_peers + plane_peers + cross_peers:
        pl.semaphore_signal(barrier, inc=1, device_id={"tile": peer}, device_id_type=pl.DeviceIdType.MESH)
    load_ice = pltpu.make_async_copy(ice, icev, ls.at[0])
    load_sens = pltpu.make_async_copy(sens, sensv, ls.at[1])
    load_cw = pltpu.make_async_copy(cw, cwv, ls.at[2])
    load_ice.start()
    load_cw.start()
    load_sens.start()

    for q in range(forc.shape[0]):
        for i in range(F):
            f2[q * 8 : q * 8 + 8, i * 128 : i * 128 + 128] = forc[q, i].astype(f32)
    fs[mine] = f2[...].astype(bf16)
    locs = slot_t[...] * forc.shape[2] + off_t[...]
    for i, x in enumerate((own_t[...].astype(f32), locs.astype(f32), w_t[...])):
        info_s[i : i + 1, :] = jnp.concatenate([x[k : k + 1, :] for k in range(K)], axis=1)
    info_s[3:4, :] = jnp.zeros((1, 128), f32)
    near[1] = info_s[...]

    def behind(j):
        return core * nz + lax.rem(z + nz - j, nz)

    pl.semaphore_wait(barrier, 2 * nz + 4)
    f_near = [
        remote(info_s, near.at[0], ss1.at[0], rs1.at[0], right), remote(info_s, near.at[2], ss1.at[1], rs1.at[1], left)
    ]
    for copy in f_near:
        copy.start()
    f_line = [remote(fs.at[mine], fs.at[mine], ss2.at[j + 1], rs2.at[j + 1], line_peers[j]) for j in range(nz - 1)]
    for copy in f_line:
        copy.start()
    f_share = [remote(fs.at[behind(j)], fs.at[behind(j)], ss4.at[j], rs4.at[j], sibling) for j in range(nz)]
    f_share[0].start()

    halos = []
    for i, (src, dst, rows) in enumerate(((ice, iceh, 6), (ocean, och, 8), (sens, sensh, 3))):
        halos.append(remote(src.at[pl.ds(ROWS_DEV - rows, rows)], dst.at[0], ss3.at[2 * i], rs3.at[2 * i], right))
        halos.append(remote(src.at[pl.ds(0, rows)], dst.at[1], ss3.at[2 * i + 1], rs3.at[2 * i + 1], left))
    for copy in halos[:4]:
        copy.start()
    tell = [remote(info_s, info.at[mine], ss1.at[2 + j], rs1.at[2 + j], line_peers[j]) for j in range(nz - 1)]
    tell += [remote(info_s, info.at[mine], ss1.at[nz + 2 + j], rs1.at[nz + 2 + j], cross_peers[j]) for j in range(nz)]
    info[mine] = info_s[...]

    keep_low = jnp.where(me == 0, 0.0, 1.0)
    keep_high = jnp.where(me == n - 1, 0.0, 1.0)
    rows = iota((128, 128), 0)
    diag = jnp.where(rows == iota((128, 128), 1), 1.0, 0.0)
    ones = jnp.ones((128, 128), bf16)
    not_first = rows > 0
    not_last = rows < 127

    def put(dst, pair, half, v):
        at = half * 384
        dst[pair, :, at : at + 128] = jnp.where(not_first, pltpu.roll(v, 1, 0), 0.0).astype(bf16)
        dst[pair, :, at + 128 : at + 256] = v.astype(bf16)
        dst[pair, :, at + 256 : at + 384] = jnp.where(not_last, pltpu.roll(v, 127, 0), 0.0).astype(bf16)

    def put_a(e, v):
        put(xa, e // 2, e % 2, v)

    def put_b(e, v):
        put(xb, (e - 1) // 2, (e - 1) % 2, v)

    def set_weights(layer):
        for s in range(2):
            at = (3 - 3 * s) * 384
            wall[layer, at : at + 384, s * 128 : s * 128 + 128] = jnp.zeros((384, 128), bf16)
        for a in range(3):
            for b in range(3):
                if layer < 3:
                    tile = cwv[layer * 9 + a * 3 + b]
                else:
                    tile = cwv[(layer - 3) * 9 + (2 - a) * 3 + 2 - b].T
                for s in range(2):
                    at = (a + s) * 384 + b * 128
                    wall[layer, at : at + 128, s * 128 : s * 128 + 128] = tile

    def spread(c, carry):
        e = 8 * c
        cells = oc[pl.ds(pl.multiple_of(e, 8), 8), :]
        wide = jnp.concatenate([(diag * cells[i : i + 1, :]).astype(bf16) for i in range(8)], axis=0)
        mask[pl.ds(e, 8)] = dot(wide, ones).reshape(8, 128, 128)
        return carry

    def stage(layer, src, q0, pairs, finish):
        odd = 0 if src is xa else 1
        lhs = src[q0 : q0 + pairs].reshape(pairs * 128, 768)
        rhs = src[q0 + 1 : q0 + 1 + pairs].reshape(pairs * 128, 768)
        acc = dot(lhs, wall[layer, 0:768, :]) + dot(rhs, wall[layer, 768:1536, :])
        for i in range(pairs):
            for s in range(2):
                finish(2 * (q0 + i) + odd + 1 + s, acc[i * 128 : i * 128 + 128, s * 128 : s * 128 + 128])

    def middle_a(e):
        return xa[e // 2, :, (e % 2) * 384 + 128 : (e % 2) * 384 + 256].astype(f32)

    def middle_b(e):
        return xb[(e - 1) // 2, :, ((e - 1) % 2) * 384 + 128 : ((e - 1) % 2) * 384 + 256].astype(f32)

    def sens_row(e):
        if e < 8:
            return sensh[0, e - 5].astype(f32)
        if e >= 40:
            return sensh[1, e - 40].astype(f32)
        return sensv[e - 8].astype(f32)

    def conv0(e, acc):
        t = jnp.tanh(acc + cb[0:1, :])
        m = mask[e]
        if 7 <= e <= 40:
            s0[e] = m * (1.0 - t * t)
        h1[e] = (middle_a(e) + m * t).astype(bf16)

    def conv1(e, acc):
        t = jnp.tanh(acc + cb[1:2, :])
        m = mask[e]
        if 6 <= e <= 41:
            s1[e] = m * (1.0 - t * t)
        put_a(e, middle_b(e) + m * t)

    def conv2(e, acc):
        t = jnp.tanh(acc + cb[2:3, :])
        m = mask[e]
        if 8 <= e < 40:
            img[e - 8] = (middle_a(e) + m * t).astype(bf16)
        put_b(e, sens_row(e) * (m * (1.0 - t * t)))

    def back2(e, acc):
        total = sens_row(e) + acc
        g[e] = total
        put_a(e, total * s1[e])

    def back1(e, acc):
        total = g[e] + acc
        g[e] = total
        put_b(e, total * s0[e])

    def back0(e, acc):
        sg[e - 8] = (g[e] + acc).astype(bf16)

    load_ice.wait()
    load_cw.wait()
    set_weights(0)
    oc[8:40, :] = ocean[...].astype(f32)
    lax.fori_loop(1, 5, spread, 0)

    def fill(q, carry):
        put(xa, q + 4, 0, icev[2 * q].astype(f32))
        put(xa, q + 4, 1, icev[2 * q + 1].astype(f32))
        return carry

    lax.fori_loop(0, ROWS_DEV // 2, fill, 0)
    for copy in f_near:
        copy.wait()
    lane, row = iota((3 * 128, 256), 1), iota((3 * 128, 256), 0)
    k, e = lane // 64, lax.rem(lane, 64)
    choose = jnp.where((e < E) & (row == (e + 24) // ROWS_DEV * 128 + k * ROWS_DEV + lax.rem(e + 24, ROWS_DEV)), 1.0, 0.0)
    own = jnp.concatenate([near[i] for i in range(3)], axis=1)
    ext_s[...] = dot(jnp.concatenate([own, jnp.zeros_like(own)], axis=0).astype(bf16), choose.astype(bf16))
    ext[0] = ext_s[...]
    f_ext = [remote(ext_s, ext.at[j + 1], ss9.at[j], rs9.at[j], plane_peers[j]) for j in range(3)]
    for copy in f_ext:
        copy.start()
    for copy in tell:
        copy.start()
    for c in range(3):
        stage(0, xa, 4 + 5 * c, 5, conv0)
    for layer in range(1, 6):
        set_weights(layer)
    l16[...] = jnp.zeros_like(l16)
    l16[0:F, :] = lift[...].astype(f32)
    lift16 = l16[...].astype(bf16)
    eight = jnp.concatenate([lift16] * 8, axis=0)
    of_row = iota((128, 128), 0) // FP
    for i in range(8):
        bd[:, i * 128 : i * 128 + 128] = jnp.where(of_row == i, eight, jnp.zeros_like(eight))
    cm = col_map[...].astype(bf16)

    def record(rec):
        owner, loc = rec[0:1, :].astype(jnp.int32), rec[1:2, :].astype(jnp.int32)
        return lax.div(owner, PLANE), lax.div(lax.rem(owner, PLANE), 2), lax.rem(owner, 2), loc, rec[2:3, :]

    for copy in f_ext:
        copy.wait()
    nf = 2 * nz * OWN
    spots = lax.rem(iota((E, 256), 1), 64) == iota((E, 256), 0)
    spots = jnp.where(spots, 1.0, 0.0).astype(bf16)
    for j in range(4):
        oz, ochip, ocore, loc, w = record(ext[(4 - j) % 4])
        at = jnp.where(ochip == chip, (ocore * nz + oz) * OWN + loc, -1)
        one = jnp.where(iota((nf, 256), 0) == at, w, 0.0).astype(bf16)
        wsum[j * E : j * E + E, :] = dot(spots, one, 1, 1).astype(bf16)

    for j in range(1, nz):
        f_line[j - 1].wait()
        f_share[j].start()

    def plane(src, dst, at, size, send, recv, first):
        return [
            remote(
                src.at[j, pl.ds(at, size)], dst.at[j, pl.ds(at, size)], send.at[first + j], recv.at[first + j],
                plane_peers[j - 1],
            )
            for j in range(1, 4)
        ]

    for copy in f_share:
        copy.wait()
    ps[...] = dot(wsum[...], fs[...].reshape(nf, WIDE)).astype(bf16).reshape(4, E, WIDE)
    f_plane = [plane(ps, pv, 16 * c, 16, ss5, rs5, 4 * c) for c in range(3)]
    for group in f_plane:
        for copy in group:
            copy.start()
    for copy in halos[4:]:
        copy.start()
    for copy in tell:
        copy.wait()

    row, lane = iota((64, 128), 0), iota((64, 128), 1)
    same = lax.rem(lane, ROWS_DEV) == row // 16 * 8 + lax.rem(row, 8)
    low = lax.rem(row, 16) < 8
    pick_low = jnp.where(same & low, 1.0, 0.0).astype(bf16)
    pick_high = jnp.where(same & ~low, 1.0, 0.0).astype(bf16)
    for c in range(2 * nz):
        oz, ochip, ocore, loc, w = record(info[c])
        at = jnp.where((oz == z) & (ocore == core), lax.rem(ochip + 4 - chip, 4) * OWN + loc, -1)
        one = jnp.where(iota((4 * OWN, 128), 0) == at, w, 0.0).astype(bf16)
        for half, pick in enumerate((pick_low, pick_high)):
            part = dot(pick, one, 1, 1).astype(bf16)
            for i in range(4):
                to = (i * 2 * nz + c) * 16
                vt[to : to + 16, half * 128 : half * 128 + 128] = part[i * 16 : i * 16 + 16]
    for copy in halos[:4]:
        copy.wait()
    oc[0:8, :] = och[0].astype(f32) * keep_low
    oc[40:48, :] = och[1].astype(f32) * keep_high
    spread(0, 0)
    spread(5, 0)
    for i in range(6):
        put_a(2 + i, iceh[0, i].astype(f32) * keep_low)
        put_a(40 + i, iceh[1, i].astype(f32) * keep_high)
    stage(0, xa, 1, 3, conv0)
    stage(0, xa, 19, 3, conv0)
    icr[...] = jnp.zeros_like(icr)

    def arrive(c):
        for copy in f_plane[c]:
            copy.wait()
        x = jnp.concatenate([
            sum((pv if j else ps)[j, 16 * c : 16 * c + 16, i * 128 : i * 128 + 128].astype(f32) for j in range(4)) for i in range(F)
        ], axis=0)
        erow = iota((16, 1), 0) + 16 * c
        inside = jnp.where(erow < 8, keep_low, jnp.where(erow < 40, 1.0, keep_high))
        y = dot(x.astype(bf16), cm)
        for i in range(F):
            icr[16 * c : 16 * c + 16, i, :] = y[16 * i : 16 * i + 16] * inside

    def lift_eight(c):
        wide = dot(icr[8 * c : 8 * c + 8].reshape(8 * FP, 128).astype(bf16), bd[...], 0, 0)
        for i in range(8):
            e = 8 * c + i
            if 3 <= e <= 44:
                put_b(e, h1[e].astype(f32) + wide[:, i * 128 : i * 128 + 128])

    def t_line(c):
        return [
            remote(prg.at[c, mine], prg.at[c, mine], ss6.at[c * nz + j], rs6.at[c * nz + j], lax.rem(z + j, nz) * PLANE + p)
            for j in range(1, nz)
        ]

    def t_share(c):
        part = prg.at[c, pl.ds(core * nz, nz)]
        return remote(part, part, ss7.at[c], rs7.at[c], sibling)

    lines, shares = [], []

    def project(c):
        wide = jnp.concatenate([g[8 * c + 8 + i].astype(bf16) for i in range(8)], axis=1)
        y = dot(dot(bd[...], wide, 1, 1).astype(bf16), cm, 1, 1)
        fg[...] = y.reshape(8, FP, 128)
        for half in range(2):
            for i in range(5):
                f3[half * 8 : half * 8 + 8, i * 128 : i * 128 + 128] = fg[:, half * 5 + i, :]
        prg[c, mine] = f3[...].astype(bf16)
        lines.append(t_line(c))
        for copy in lines[c]:
            copy.start()

    def relay(c):
        for copy in lines[c]:
            copy.wait()
        shares.append(t_share(c))
        shares[c].start()

    layers = {1: (1, xb, 1, conv1), 2: (2, xa, 2, conv2), 3: (5, xb, 2, back2), 4: (4, xa, 3, back1), 5: (3, xb, 3, back0)}

    def sens_ready():
        load_sens.wait()
        for copy in halos[4:]:
            copy.wait()

    events = {"arrive": arrive, "lift": lift_eight, "sens": sens_ready, "project": project, "relay": relay}
    for name, *rest in PLAN:
        if name == "conv":
            which, k0, count = rest
            layer, src, q, finish = layers[which]
            stage(layer, src, k0 + q, count, finish)
        else:
            events[name](*rest)
    for copy in shares:
        copy.wait()
    total = dot(vt[...], prg[...].reshape(2 * nf, HALF), 0, 0).astype(bf16)
    ts[:, 0:OWN, :] = total[0 : 4 * OWN].reshape(4, OWN, HALF)
    ts[:, OWN : 2 * OWN, :] = total[4 * OWN : 8 * OWN].reshape(4, OWN, HALF)
    t_plane = plane(ts, tr, 0, 2 * OWN, ss8, rs8, 0)
    for copy in t_plane:
        copy.start()
    for copy in t_plane:
        copy.wait()
    for half in range(2):
        for i in range(5):
            x = sum((tr if j else ts)[j, half * OWN : half * OWN + OWN, i * 128 : i * 128 + 128].astype(f32) for j in range(4))
            for q in range(grad.shape[0]):
                grad[q, half * 5 + i] = x[q * 8 : q * 8 + 8]


def deliver_kernel(img, sg, grad, img_out, sg_out, grad_out, sems):
    copies = [
        pltpu.make_async_copy(src, dst, sems.at[i])
        for i, (src, dst) in enumerate(((img, img_out), (sg, sg_out), (grad, grad_out)))
    ]
    for copy in copies:
        copy.start()
    for copy in copies:
        copy.wait()


def body(
    forcing, ice_state, sensitivity, owner_device, panel_slot, row_offset,
    intersection_weight, col_map, ocean_mask, lift_weight, conv_weight, conv_bias,
):
    n = lax.axis_size("tile")
    nz = n // PLANE
    nf = 2 * nz * OWN
    V, D = pltpu.VMEM, pltpu.SemaphoreType.DMA
    vmem, hbm = pl.BlockSpec(memory_space=pltpu.VMEM), pl.BlockSpec(memory_space=pl.ANY)
    panels, pr = forcing.shape[:2]
    field = (E, 128, 128)
    tile = (ROWS_DEV, 128, 128)
    shapes = [
        jax.ShapeDtypeStruct(tile, bf16),
        jax.ShapeDtypeStruct(tile, bf16),
        jax.ShapeDtypeStruct((panels, F, pr, 128), f32),
    ]
    results = pl.pallas_call(
        functools.partial(program_kernel, n),
        out_shape=shapes,
        in_specs=[hbm, hbm] + [vmem] * 8 + [hbm, vmem],
        out_specs=[vmem, vmem, vmem],
        scratch_shapes=[
            V((4, 128), f32), V((2 * nz, 4, 128), f32), V((3, 4, 128), f32), V((8, 256), f32), V((4, 8, 256), f32),
            V((OWN, WIDE), f32), V((16, HALF), f32),
            V((2 * nz, OWN, WIDE), bf16), V((4 * E, nf), bf16),
            V((4, E, WIDE), bf16), V((4, E, WIDE), bf16), V((4, 2 * nz, 16, HALF), bf16), V((2 * nf, 256), bf16),
            V((4, 2 * OWN, HALF), bf16), V((4, 2 * OWN, HALF), bf16), V((FP, 128), f32),
            V((2, 6, 128, 128), bf16), V((2, 3, 128, 128), bf16), V((2, 8, 128), jnp.int32),
            V((E // 2, 128, 768), bf16), V((E // 2, 128, 768), bf16), V(field, f32), V(field, f32),
            V(field, f32), V(field, f32), V(field, bf16),
            V((6, 1536, 256), bf16), V((E, 128), f32), V((E, FP, 128), f32), V((8, FP, 128), f32),
            V(tile, bf16), V(tile, bf16), V((27, 128, 128), bf16), V((128, 1024), bf16),
            D((2 * nz + 2,)), D((2 * nz + 2,)), D((nz,)), D((nz,)), D((6,)), D((6,)), D((nz,)), D((nz,)), D((12,)), D((12,)),
            D((4 * nz,)), D((4 * nz,)), D((4,)), D((4,)), D((4,)), D((4,)), D((3,)), D((3,)), D((3,)),
        ],
        compiler_params=pltpu.CompilerParams(
            vmem_limit_bytes=56 * 1024 * 1024, collective_id=1, has_side_effects=True
        ),
    )(ice_state, sensitivity, ocean_mask, owner_device.T, panel_slot.T, row_offset.T, intersection_weight.T,
      forcing.transpose(0, 2, 1, 3), col_map, lift_weight, conv_weight.reshape(27, 128, 128), conv_bias)
    img, sg, grad = pl.pallas_call(
        deliver_kernel,
        out_shape=shapes,
        in_specs=[vmem, vmem, vmem],
        out_specs=[hbm, hbm, hbm],
        scratch_shapes=[D((3,))],
    )(*results)
    return img, sg, grad.transpose(0, 2, 1, 3)


def solution(mesh):
    in_specs = (
        P(("member", "tile"), None, None, None),
        P(("member", "tile"), None, None),
        P(("member", "tile"), None, None),
        P("tile", None),
        P("tile", None),
        P("tile", None),
        P("tile", None),
        P(),
        P("tile", None),
        P(),
        P(),
        P(),
    )
    out_specs = (
        P(("member", "tile"), None, None),
        P(("member", "tile"), None, None),
        P(("member", "tile"), None, None, None),
    )
    return jax.shard_map(body, mesh=mesh, in_specs=in_specs, out_specs=out_specs, check_vma=False)
```

```python
import functools

import jax
import jax.numpy as jnp
from jax import lax
from jax.experimental import pallas as pl
from jax.experimental.pallas import tpu as pltpu
from jax.sharding import PartitionSpec as P

F = 10
K = 4
ROWS_DEV = 32
FP = 16
PLANE = 8
OWN = 32
WIDE = F * 128
HALF = WIDE // 2
E = 48
STEP = 4
f32, bf16 = jnp.float32, jnp.bfloat16

PLAN = (
    ('arrive', 0),
    ('lift', 0),
    ('lift', 1),
    ('conv', 1, 0, 4),
    ('arrive', 1),
    ('lift', 2),
    ('sens',),
    ('conv', 2, 0, 3),
    ('conv', 1, 4, 4),
    ('lift', 3),
    ('conv', 3, 0, 2),
    ('conv', 2, 3, 4),
    ('conv', 1, 8, 4),
    ('arrive', 2),
    ('lift', 4),
    ('conv', 4, 0, 1),
    ('conv', 3, 2, 4),
    ('conv', 2, 7, 4),
    ('conv', 1, 12, 4),
    ('lift', 5),
    ('conv', 4, 1, 4),
    ('conv', 3, 6, 4),
    ('conv', 2, 11, 4),
    ('conv', 1, 16, 4),
    ('project', 0),
    ('conv', 4, 5, 4),
    ('conv', 3, 10, 4),
    ('conv', 2, 15, 4),
    ('project', 1),
    ('conv', 4, 9, 4),
    ('conv', 3, 14, 4),
    ('project', 2),
    ('conv', 4, 13, 4),
    ('project', 3),
    ('relay', 0),
    ('relay', 1),
    ('back0', 0, 4),
    ('relay', 2),
    ('relay', 3),
)


def dot(a, b, ca=1, cb=0):
    return lax.dot_general(a, b, (((ca,), (cb,)), ((), ())), preferred_element_type=f32)


def iota(shape, dim):
    return lax.broadcasted_iota(jnp.int32, shape, dim)


def remote(src, dst, send, recv, target):
    return pltpu.make_async_remote_copy(
        src_ref=src, dst_ref=dst, send_sem=send, recv_sem=recv,
        device_id={"tile": target}, device_id_type=pl.DeviceIdType.MESH,
    )


def program_kernel(
    n, ice, sens, ocean_h, own_h, slot_h, off_h, w_h, forc_h, col_h, lift_h, cw, cb_h,
    img, sg, grad,
    info_s, info, near, ext_s, ext, f2, f3, fs, wsum, ps, pv, prg, vt, ts, tr, l16, iceh, sensh, och,
    xa, xb, s0, s1, mask, g, h1, wall, oc, icr, fg, icev, sensv, cwv, bd,
    ss1, rs1, ss2, rs2, ss3, rs3, ss4, rs4, ss5, rs5, ss6, rs6, ss7, rs7, ss8, rs8, ss9, rs9, ls,
    ocean, own_t, slot_t, off_t, w_t, forc, col_map, lift, cb,
):
    me = lax.axis_index("tile")
    right, left = lax.rem(me + 1, n), lax.rem(me + n - 1, n)
    nz = n // PLANE
    z, p = lax.div(me, PLANE), lax.rem(me, PLANE)
    chip, core = lax.div(p, 2), lax.rem(p, 2)
    sibling = me + 1 - 2 * core
    mine = core * nz + z
    barrier = pltpu.get_barrier_semaphore()

    line_peers = [lax.rem(z + j, nz) * PLANE + p for j in range(1, nz)]
    plane_peers = [z * PLANE + lax.rem(chip + j, 4) * 2 + core for j in range(1, 4)]
    cross_peers = [lax.rem(z + j, nz) * PLANE + p + 1 - 2 * core for j in range(nz)]
    for peer in [left, right] + line_peers + plane_peers + cross_peers:
        pl.semaphore_signal(barrier, inc=1, device_id={"tile": peer}, device_id_type=pl.DeviceIdType.MESH)
    load_ice = pltpu.make_async_copy(ice, icev, ls.at[0])
    load_sens = pltpu.make_async_copy(sens, sensv, ls.at[1])
    load_cw = pltpu.make_async_copy(cw, cwv, ls.at[2])
    small = [
        pltpu.make_async_copy(src, dst, ls.at[3 + i])
        for i, (src, dst) in enumerate((
            (forc_h, forc), (own_h, own_t), (slot_h, slot_t), (off_h, off_t), (w_h, w_t), (ocean_h, ocean),
            (col_h, col_map), (lift_h, lift), (cb_h, cb),
        ))
    ]
    for copy in small:
        copy.start()
    load_ice.start()
    load_cw.start()
    load_sens.start()
    for copy in small:
        copy.wait()

    for q in range(forc.shape[0]):
        for i in range(F):
            f2[q * 8 : q * 8 + 8, i * 128 : i * 128 + 128] = forc[q, i].astype(f32)
    fs[mine] = f2[...].astype(bf16)
    locs = slot_t[...] * forc.shape[2] + off_t[...]
    for i, x in enumerate((own_t[...].astype(f32), locs.astype(f32), w_t[...])):
        info_s[i : i + 1, :] = jnp.concatenate([x[k : k + 1, :] for k in range(K)], axis=1)
    info_s[3:4, :] = jnp.zeros((1, 128), f32)
    near[1] = info_s[...]

    def behind(j):
        return core * nz + lax.rem(z + nz - j, nz)

    pl.semaphore_wait(barrier, 2 * nz + 4)
    f_near = [
        remote(info_s, near.at[0], ss1.at[0], rs1.at[0], right), remote(info_s, near.at[2], ss1.at[1], rs1.at[1], left)
    ]
    for copy in f_near:
        copy.start()
    f_line = [remote(fs.at[mine], fs.at[mine], ss2.at[j + 1], rs2.at[j + 1], line_peers[j]) for j in range(nz - 1)]
    for copy in f_line:
        copy.start()
    f_share = [remote(fs.at[behind(j)], fs.at[behind(j)], ss4.at[j], rs4.at[j], sibling) for j in range(nz)]
    f_share[0].start()

    halos = []
    for i, (src, dst, rows) in enumerate(((ice, iceh, 6), (ocean_h, och, 8), (sens, sensh, 3))):
        halos.append(remote(src.at[pl.ds(ROWS_DEV - rows, rows)], dst.at[0], ss3.at[2 * i], rs3.at[2 * i], right))
        halos.append(remote(src.at[pl.ds(0, rows)], dst.at[1], ss3.at[2 * i + 1], rs3.at[2 * i + 1], left))
    up_now, down_now = p != PLANE - 1, p != 0

    def start_halos(up, down, which):
        @pl.when(up)
        def _():
            for i in which:
                halos[2 * i].start()

        @pl.when(down)
        def _():
            for i in which:
                halos[2 * i + 1].start()

    start_halos(up_now, down_now, (0, 1, 2))
    tell = [remote(info_s, info.at[mine], ss1.at[2 + j], rs1.at[2 + j], line_peers[j]) for j in range(nz - 1)]
    tell += [remote(info_s, info.at[mine], ss1.at[nz + 2 + j], rs1.at[nz + 2 + j], cross_peers[j]) for j in range(nz)]
    info[mine] = info_s[...]

    keep_low = jnp.where(me == 0, 0.0, 1.0)
    keep_high = jnp.where(me == n - 1, 0.0, 1.0)
    rows = iota((128, 128), 0)
    diag = jnp.where(rows == iota((128, 128), 1), 1.0, 0.0)
    ones = jnp.ones((128, 128), bf16)
    not_first = rows > 0
    not_last = rows < 127

    def put(dst, pair, half, v):
        at = half * 384
        dst[pair, :, at : at + 128] = jnp.where(not_first, pltpu.roll(v, 1, 0), 0.0).astype(bf16)
        dst[pair, :, at + 128 : at + 256] = v.astype(bf16)
        dst[pair, :, at + 256 : at + 384] = jnp.where(not_last, pltpu.roll(v, 127, 0), 0.0).astype(bf16)

    def put_a(e, v):
        put(xa, e // 2, e % 2, v)

    def put_b(e, v):
        put(xb, (e - 1) // 2, (e - 1) % 2, v)

    def set_weights(layer):
        for s in range(2):
            at = (3 - 3 * s) * 384
            wall[layer, at : at + 384, s * 128 : s * 128 + 128] = jnp.zeros((384, 128), bf16)
        for a in range(3):
            for b in range(3):
                if layer < 3:
                    tile = cwv[layer * 9 + a * 3 + b]
                else:
                    tile = cwv[(layer - 3) * 9 + (2 - a) * 3 + 2 - b].T
                for s in range(2):
                    at = (a + s) * 384 + b * 128
                    wall[layer, at : at + 128, s * 128 : s * 128 + 128] = tile

    def spread(c, carry):
        e = 8 * c
        cells = oc[pl.ds(pl.multiple_of(e, 8), 8), :]
        wide = jnp.concatenate([(diag * cells[i : i + 1, :]).astype(bf16) for i in range(8)], axis=0)
        mask[pl.ds(e, 8)] = dot(wide, ones).reshape(8, 128, 128)
        return carry

    def stage(layer, src, q0, pairs, finish):
        odd = 0 if src is xa else 1
        lhs = src[pl.ds(q0, pairs)].reshape(pairs * 128, 768)
        rhs = src[pl.ds(q0 + 1, pairs)].reshape(pairs * 128, 768)
        acc = dot(lhs, wall[layer, 0:768, :]) + dot(rhs, wall[layer, 768:1536, :])
        for i in range(pairs):
            for s in range(2):
                finish(2 * (q0 + i) + odd + 1 + s, acc[i * 128 : i * 128 + 128, s * 128 : s * 128 + 128])

    def middle_a(e):
        return xa[e // 2, :, (e % 2) * 384 + 128 : (e % 2) * 384 + 256].astype(f32)

    def middle_b(e):
        return xb[(e - 1) // 2, :, ((e - 1) % 2) * 384 + 128 : ((e - 1) % 2) * 384 + 256].astype(f32)

    def sens_row(e):
        if e < 8:
            return sensh[0, e - 5].astype(f32)
        if e >= 40:
            return sensh[1, e - 40].astype(f32)
        return sensv[e - 8].astype(f32)

    def conv0(e, acc):
        t = jnp.tanh(acc + cb[0:1, :])
        m = mask[e]
        if 7 <= e <= 40:
            s0[e] = m * (1.0 - t * t)
        h1[e] = (middle_a(e) + m * t).astype(bf16)

    def conv1(e, acc):
        t = jnp.tanh(acc + cb[1:2, :])
        m = mask[e]
        if 6 <= e <= 41:
            s1[e] = m * (1.0 - t * t)
        put_a(e, middle_b(e) + m * t)

    def conv2(e, acc):
        t = jnp.tanh(acc + cb[2:3, :])
        m = mask[e]
        if 8 <= e < 40:
            img[e - 8] = (middle_a(e) + m * t).astype(bf16)
        put_b(e, sens_row(e) * (m * (1.0 - t * t)))

    def back2(e, acc):
        total = sens_row(e) + acc
        g[e] = total
        put_a(e, total * s1[e])

    def back1(e, acc):
        total = g[e] + acc
        g[e] = total
        put_b(e, total * s0[e])

    def back0(e, acc):
        sg[e - 8] = (g[e] + acc).astype(bf16)

    load_ice.wait()
    load_cw.wait()
    set_weights(0)
    oc[8:40, :] = ocean[...].astype(f32)
    lax.fori_loop(1, 5, spread, 0)

    def fill(q, carry):
        put(xa, q + 4, 0, icev[2 * q].astype(f32))
        put(xa, q + 4, 1, icev[2 * q + 1].astype(f32))
        return carry

    lax.fori_loop(0, ROWS_DEV // 2, fill, 0)
    for copy in f_near:
        copy.wait()
    lane, row = iota((3 * 128, 256), 1), iota((3 * 128, 256), 0)
    k, e = lane // 64, lax.rem(lane, 64)
    choose = jnp.where((e < E) & (row == (e + 24) // ROWS_DEV * 128 + k * ROWS_DEV + lax.rem(e + 24, ROWS_DEV)), 1.0, 0.0)
    own = jnp.concatenate([near[i] for i in range(3)], axis=1)
    ext_s[...] = dot(jnp.concatenate([own, jnp.zeros_like(own)], axis=0).astype(bf16), choose.astype(bf16))
    ext[0] = ext_s[...]
    f_ext = [remote(ext_s, ext.at[j + 1], ss9.at[j], rs9.at[j], plane_peers[j]) for j in range(3)]
    for copy in f_ext:
        copy.start()
    for copy in tell:
        copy.start()
    def inner0(c, carry):
        q0 = 4 + 5 * c
        lhs = xa[pl.ds(q0, 5)].reshape(5 * 128, 768)
        rhs = xa[pl.ds(q0 + 1, 5)].reshape(5 * 128, 768)
        acc = dot(lhs, wall[0, 0:768, :]) + dot(rhs, wall[0, 768:1536, :])
        for i in range(5):
            for s in range(2):
                e = 2 * (q0 + i) + 1 + s
                t = jnp.tanh(acc[i * 128 : i * 128 + 128, s * 128 : s * 128 + 128] + cb[0:1, :])
                m = mask[e]
                s0[e] = m * (1.0 - t * t)
                at = (1 - s) * 384 + 128
                h1[e] = (xa[q0 + i + s, :, at : at + 128].astype(f32) + m * t).astype(bf16)
        return carry

    lax.fori_loop(0, 3, inner0, 0)
    for layer in range(1, 6):
        set_weights(layer)
    l16[...] = jnp.zeros_like(l16)
    l16[0:F, :] = lift[...].astype(f32)
    lift16 = l16[...].astype(bf16)
    eight = jnp.concatenate([lift16] * 8, axis=0)
    of_row = iota((128, 128), 0) // FP
    for i in range(8):
        bd[:, i * 128 : i * 128 + 128] = jnp.where(of_row == i, eight, jnp.zeros_like(eight))
    cm = col_map[...].astype(bf16)

    def record(rec):
        owner, loc = rec[0:1, :].astype(jnp.int32), rec[1:2, :].astype(jnp.int32)
        return lax.div(owner, PLANE), lax.div(lax.rem(owner, PLANE), 2), lax.rem(owner, 2), loc, rec[2:3, :]

    for copy in f_ext:
        copy.wait()
    nf = 2 * nz * OWN
    spots = lax.rem(iota((E, 256), 1), 64) == iota((E, 256), 0)
    spots = jnp.where(spots, 1.0, 0.0).astype(bf16)
    for j in range(4):
        oz, ochip, ocore, loc, w = record(ext[(4 - j) % 4])
        at = jnp.where(ochip == chip, (ocore * nz + oz) * OWN + loc, -1)
        one = jnp.where(iota((nf, 256), 0) == at, w, 0.0).astype(bf16)
        wsum[j * E : j * E + E, :] = dot(spots, one, 1, 1).astype(bf16)

    for j in range(1, nz):
        f_line[j - 1].wait()
        f_share[j].start()

    def plane(src, dst, at, size, send, recv, first):
        return [
            remote(
                src.at[j, pl.ds(at, size)], dst.at[j, pl.ds(at, size)], send.at[first + j], recv.at[first + j],
                plane_peers[j - 1],
            )
            for j in range(1, 4)
        ]

    start_halos(p == PLANE - 1, p == 0, (0, 1, 2))
    for copy in f_share:
        copy.wait()
    ps[...] = dot(wsum[...], fs[...].reshape(nf, WIDE)).astype(bf16).reshape(4, E, WIDE)
    f_plane = [plane(ps, pv, 16 * c, 16, ss5, rs5, 4 * c) for c in range(3)]
    for copy in f_plane[0]:
        copy.start()
    for copy in tell:
        copy.wait()

    row, lane = iota((64, 128), 0), iota((64, 128), 1)
    same = lax.rem(lane, ROWS_DEV) == row // 16 * 8 + lax.rem(row, 8)
    low = lax.rem(row, 16) < 8
    pick_low = jnp.where(same & low, 1.0, 0.0).astype(bf16)
    pick_high = jnp.where(same & ~low, 1.0, 0.0).astype(bf16)
    for c in range(2 * nz):
        oz, ochip, ocore, loc, w = record(info[c])
        at = jnp.where((oz == z) & (ocore == core), lax.rem(ochip + 4 - chip, 4) * OWN + loc, -1)
        one = jnp.where(iota((4 * OWN, 128), 0) == at, w, 0.0).astype(bf16)
        for half, pick in enumerate((pick_low, pick_high)):
            part = dot(pick, one, 1, 1).astype(bf16)
            for i in range(4):
                to = (i * 2 * nz + c) * 16
                vt[to : to + 16, half * 128 : half * 128 + 128] = part[i * 16 : i * 16 + 16]
    for copy in f_plane[1]:
        copy.start()
    for copy in halos[:4]:
        copy.wait()
    oc[0:8, :] = och[0].astype(f32) * keep_low
    oc[40:48, :] = och[1].astype(f32) * keep_high
    spread(0, 0)
    spread(5, 0)
    for i in range(6):
        put_a(2 + i, iceh[0, i].astype(f32) * keep_low)
        put_a(40 + i, iceh[1, i].astype(f32) * keep_high)
    stage(0, xa, 1, 3, conv0)
    stage(0, xa, 19, 3, conv0)
    icr[...] = jnp.zeros_like(icr)

    def arrive(c):
        for copy in f_plane[c]:
            copy.wait()
        if c == 0:
            for copy in f_plane[2]:
                copy.start()
        x = jnp.concatenate([
            sum((pv if j else ps)[j, 16 * c : 16 * c + 16, i * 128 : i * 128 + 128].astype(f32) for j in range(4)) for i in range(F)
        ], axis=0)
        erow = iota((16, 1), 0) + 16 * c
        inside = jnp.where(erow < 8, keep_low, jnp.where(erow < 40, 1.0, keep_high))
        y = dot(x.astype(bf16), cm)
        for i in range(F):
            icr[16 * c : 16 * c + 16, i, :] = y[16 * i : 16 * i + 16] * inside

    def lift_eight(c):
        wide = dot(icr[8 * c : 8 * c + 8].reshape(8 * FP, 128).astype(bf16), bd[...], 0, 0)
        for i in range(8):
            e = 8 * c + i
            if 3 <= e <= 44:
                put_b(e, h1[e].astype(f32) + wide[:, i * 128 : i * 128 + 128])

    def t_line(c):
        return [
            remote(prg.at[c, mine], prg.at[c, mine], ss6.at[c * nz + j], rs6.at[c * nz + j], lax.rem(z + j, nz) * PLANE + p)
            for j in range(1, nz)
        ]

    def t_share(c):
        part = prg.at[c, pl.ds(core * nz, nz)]
        return remote(part, part, ss7.at[c], rs7.at[c], sibling)

    lines, shares = [], []

    def project(c):
        wide = jnp.concatenate([g[8 * c + 8 + i].astype(bf16) for i in range(8)], axis=1)
        y = dot(dot(bd[...], wide, 1, 1).astype(bf16), cm, 1, 1)
        fg[...] = y.reshape(8, FP, 128)
        for half in range(2):
            for i in range(5):
                f3[half * 8 : half * 8 + 8, i * 128 : i * 128 + 128] = fg[:, half * 5 + i, :]
        prg[c, mine] = f3[...].astype(bf16)
        lines.append(t_line(c))
        for copy in lines[c]:
            copy.start()

    def relay(c):
        for copy in lines[c]:
            copy.wait()
        shares.append(t_share(c))
        shares[c].start()

    layers = {1: (1, xb, 1, conv1), 2: (2, xa, 2, conv2), 3: (5, xb, 2, back2), 4: (4, xa, 3, back1), 5: (3, xb, 3, back0)}

    def sens_ready():
        load_sens.wait()
        for copy in halos[4:]:
            copy.wait()

    def back0_loop(first, count):
        def body(i, carry):
            stage(3, xb, 3 + first + STEP * i, STEP, back0)
            return carry

        lax.fori_loop(0, count, body, 0)

    events = {"back0": back0_loop, "arrive": arrive, "lift": lift_eight, "sens": sens_ready, "project": project, "relay": relay}
    for name, *rest in PLAN:
        if name == "conv":
            which, k0, count = rest
            layer, src, q, finish = layers[which]
            stage(layer, src, k0 + q, count, finish)
        else:
            events[name](*rest)
    for copy in shares:
        copy.wait()
    total = dot(vt[...], prg[...].reshape(2 * nf, HALF), 0, 0).astype(bf16)
    ts[:, 0:OWN, :] = total[0 : 4 * OWN].reshape(4, OWN, HALF)
    ts[:, OWN : 2 * OWN, :] = total[4 * OWN : 8 * OWN].reshape(4, OWN, HALF)
    t_plane = plane(ts, tr, 0, 2 * OWN, ss8, rs8, 0)
    for copy in t_plane:
        copy.start()
    for copy in t_plane:
        copy.wait()
    for half in range(2):
        for i in range(5):
            x = sum((tr if j else ts)[j, half * OWN : half * OWN + OWN, i * 128 : i * 128 + 128].astype(f32) for j in range(4))
            for q in range(grad.shape[0]):
                grad[q, half * 5 + i] = x[q * 8 : q * 8 + 8]


def deliver_kernel(img, sg, grad, img_out, sg_out, grad_out, sems):
    copies = [
        pltpu.make_async_copy(src, dst, sems.at[i])
        for i, (src, dst) in enumerate(((img, img_out), (sg, sg_out), (grad, grad_out)))
    ]
    for copy in copies:
        copy.start()
    for copy in copies:
        copy.wait()


def body(
    forcing, ice_state, sensitivity, owner_device, panel_slot, row_offset,
    intersection_weight, col_map, ocean_mask, lift_weight, conv_weight, conv_bias,
):
    n = lax.axis_size("tile")
    nz = n // PLANE
    nf = 2 * nz * OWN
    V, D = pltpu.VMEM, pltpu.SemaphoreType.DMA
    vmem, hbm = pl.BlockSpec(memory_space=pltpu.VMEM), pl.BlockSpec(memory_space=pl.ANY)
    panels, pr = forcing.shape[:2]
    field = (E, 128, 128)
    tile = (ROWS_DEV, 128, 128)
    shapes = [
        jax.ShapeDtypeStruct(tile, bf16),
        jax.ShapeDtypeStruct(tile, bf16),
        jax.ShapeDtypeStruct((panels, F, pr, 128), f32),
    ]
    results = pl.pallas_call(
        functools.partial(program_kernel, n),
        out_shape=[pltpu.VMEM(x.shape, x.dtype) for x in shapes],
        in_specs=[hbm] * 12,
        out_specs=[vmem, vmem, vmem],
        scratch_shapes=[
            V((4, 128), f32), V((2 * nz, 4, 128), f32), V((3, 4, 128), f32), V((8, 256), f32), V((4, 8, 256), f32),
            V((OWN, WIDE), f32), V((16, HALF), f32),
            V((2 * nz, OWN, WIDE), bf16), V((4 * E, nf), bf16),
            V((4, E, WIDE), bf16), V((4, E, WIDE), bf16), V((4, 2 * nz, 16, HALF), bf16), V((2 * nf, 256), bf16),
            V((4, 2 * OWN, HALF), bf16), V((4, 2 * OWN, HALF), bf16), V((FP, 128), f32),
            V((2, 6, 128, 128), bf16), V((2, 3, 128, 128), bf16), V((2, 8, 128), jnp.int32),
            V((E // 2, 128, 768), bf16), V((E // 2, 128, 768), bf16), V(field, f32), V(field, f32),
            V(field, f32), V(field, f32), V(field, bf16),
            V((6, 1536, 256), bf16), V((E, 128), f32), V((E, FP, 128), f32), V((8, FP, 128), f32),
            V(tile, bf16), V(tile, bf16), V((27, 128, 128), bf16), V((128, 1024), bf16),
            D((2 * nz + 2,)), D((2 * nz + 2,)), D((nz,)), D((nz,)), D((6,)), D((6,)), D((nz,)), D((nz,)), D((12,)), D((12,)),
            D((4 * nz,)), D((4 * nz,)), D((4,)), D((4,)), D((4,)), D((4,)), D((3,)), D((3,)), D((12,)),
            V((ROWS_DEV, 128), jnp.int32), V((K, ROWS_DEV), jnp.int32), V((K, ROWS_DEV), jnp.int32), V((K, ROWS_DEV), jnp.int32),
            V((K, ROWS_DEV), f32), V((panels, F, pr, 128), bf16), V((128, 128), f32), V((F, 128), bf16), V((3, 128), f32),
        ],
        compiler_params=pltpu.CompilerParams(
            vmem_limit_bytes=56 * 1024 * 1024, collective_id=1, has_side_effects=True
        ),
    )(ice_state, sensitivity, ocean_mask, owner_device.T, panel_slot.T, row_offset.T, intersection_weight.T,
      forcing.transpose(0, 2, 1, 3), col_map, lift_weight, conv_weight.reshape(27, 128, 128), conv_bias)
    img, sg, grad = pl.pallas_call(
        deliver_kernel,
        out_shape=shapes,
        in_specs=[vmem, vmem, vmem],
        out_specs=[hbm, hbm, hbm],
        scratch_shapes=[D((3,))],
    )(*[pltpu.with_memory_space_constraint(x, pltpu.VMEM) for x in results])
    return img, sg, grad.transpose(0, 2, 1, 3)


def solution(mesh):
    in_specs = (
        P(("member", "tile"), None, None, None),
        P(("member", "tile"), None, None),
        P(("member", "tile"), None, None),
        P("tile", None),
        P("tile", None),
        P("tile", None),
        P("tile", None),
        P(),
        P("tile", None),
        P(),
        P(),
        P(),
    )
    out_specs = (
        P(("member", "tile"), None, None),
        P(("member", "tile"), None, None),
        P(("member", "tile"), None, None, None),
    )
    return jax.shard_map(body, mesh=mesh, in_specs=in_specs, out_specs=out_specs, check_vma=False)
```

```python
import functools

import jax
import jax.numpy as jnp
from jax import lax
from jax.experimental import pallas as pl
from jax.experimental.pallas import tpu as pltpu
from jax.sharding import PartitionSpec as P

F = 10
K = 4
ROWS_DEV = 32
FP = 16
PLANE = 8
OWN = 32
WIDE = F * 128
HALF = WIDE // 2
E = 48
STEP = 4
f32, bf16 = jnp.float32, jnp.bfloat16

PLAN = (
    ('arrive', 0),
    ('lift', 0),
    ('lift', 1),
    ('conv', 1, 0, 2),
    ('sens',),
    ('conv', 2, 0, 1),
    ('conv', 1, 2, 2),
    ('arrive', 1),
    ('lift', 2),
    ('conv', 2, 1, 2),
    ('conv', 1, 4, 2),
    ('conv', 3, 0, 2),
    ('conv', 2, 3, 2),
    ('conv', 1, 6, 2),
    ('lift', 3),
    ('conv', 4, 0, 1),
    ('conv', 3, 2, 2),
    ('conv', 2, 5, 2),
    ('conv', 1, 8, 2),
    ('conv', 4, 1, 2),
    ('conv', 3, 4, 2),
    ('conv', 2, 7, 2),
    ('conv', 1, 10, 2),
    ('arrive', 2),
    ('lift', 4),
    ('conv', 4, 3, 2),
    ('project', 0),
    ('conv', 3, 6, 2),
    ('conv', 2, 9, 2),
    ('conv', 1, 12, 2),
    ('conv', 4, 5, 2),
    ('conv', 3, 8, 2),
    ('conv', 2, 11, 2),
    ('conv', 1, 14, 2),
    ('lift', 5),
    ('conv', 4, 7, 2),
    ('project', 1),
    ('conv', 3, 10, 2),
    ('conv', 2, 13, 2),
    ('conv', 1, 16, 2),
    ('conv', 4, 9, 2),
    ('conv', 3, 12, 2),
    ('conv', 2, 15, 2),
    ('conv', 1, 18, 2),
    ('conv', 4, 11, 2),
    ('project', 2),
    ('conv', 3, 14, 2),
    ('conv', 2, 17, 2),
    ('conv', 4, 13, 2),
    ('conv', 3, 16, 2),
    ('conv', 4, 15, 2),
    ('project', 3),
    ('relay', 0),
    ('relay', 1),
    ('back0', 0, 4),
    ('relay', 2),
    ('relay', 3),
)


def dot(a, b, ca=1, cb=0):
    return lax.dot_general(a, b, (((ca,), (cb,)), ((), ())), preferred_element_type=f32)


def iota(shape, dim):
    return lax.broadcasted_iota(jnp.int32, shape, dim)


def remote(src, dst, send, recv, target):
    return pltpu.make_async_remote_copy(
        src_ref=src, dst_ref=dst, send_sem=send, recv_sem=recv,
        device_id={"tile": target}, device_id_type=pl.DeviceIdType.MESH,
    )


def program_kernel(
    n, ice, sens, ocean_h, own_h, slot_h, off_h, w_h, forc_h, col_h, lift_h, cw, cb_h,
    img, sg, grad,
    info_s, info, near, ext_s, ext, f2, f3, fs, wsum, ps, pv, prg, vt, ts, tr, l16, iceh, sensh, och,
    xa, xb, s0, s1, mask, g, h1, wall, oc, icr, fg, icev, sensv, cwv, bd,
    ss1, rs1, ss2, rs2, ss3, rs3, ss4, rs4, ss5, rs5, ss6, rs6, ss7, rs7, ss8, rs8, ss9, rs9, ls,
    ocean, own_t, slot_t, off_t, w_t, forc, col_map, lift, cb,
):
    me = lax.axis_index("tile")
    right, left = lax.rem(me + 1, n), lax.rem(me + n - 1, n)
    nz = n // PLANE
    z, p = lax.div(me, PLANE), lax.rem(me, PLANE)
    chip, core = lax.div(p, 2), lax.rem(p, 2)
    sibling = me + 1 - 2 * core
    mine = core * nz + z
    barrier = pltpu.get_barrier_semaphore()

    line_peers = [lax.rem(z + j, nz) * PLANE + p for j in range(1, nz)]
    plane_peers = [z * PLANE + lax.rem(chip + j, 4) * 2 + core for j in range(1, 4)]
    cross_peers = [lax.rem(z + j, nz) * PLANE + p + 1 - 2 * core for j in range(nz)]
    for peer in [left, right] + line_peers + plane_peers + cross_peers:
        pl.semaphore_signal(barrier, inc=1, device_id={"tile": peer}, device_id_type=pl.DeviceIdType.MESH)
    load_ice = pltpu.make_async_copy(ice, icev, ls.at[0])
    load_sens = pltpu.make_async_copy(sens, sensv, ls.at[1])
    load_cw = pltpu.make_async_copy(cw, cwv, ls.at[2])
    small = [
        pltpu.make_async_copy(src, dst, ls.at[3 + i])
        for i, (src, dst) in enumerate((
            (forc_h, forc), (own_h, own_t), (slot_h, slot_t), (off_h, off_t), (w_h, w_t), (ocean_h, ocean),
            (col_h, col_map), (lift_h, lift), (cb_h, cb),
        ))
    ]
    for copy in small:
        copy.start()
    load_ice.start()
    load_cw.start()
    load_sens.start()
    for copy in small:
        copy.wait()

    for q in range(forc.shape[0]):
        for i in range(F):
            f2[q * 8 : q * 8 + 8, i * 128 : i * 128 + 128] = forc[q, i].astype(f32)
    fs[mine] = f2[...].astype(bf16)
    locs = slot_t[...] * forc.shape[2] + off_t[...]
    for i, x in enumerate((own_t[...].astype(f32), locs.astype(f32), w_t[...])):
        info_s[i : i + 1, :] = jnp.concatenate([x[k : k + 1, :] for k in range(K)], axis=1)
    info_s[3:4, :] = jnp.zeros((1, 128), f32)
    near[1] = info_s[...]

    def behind(j):
        return core * nz + lax.rem(z + nz - j, nz)

    pl.semaphore_wait(barrier, 2 * nz + 4)
    f_near = [
        remote(info_s, near.at[0], ss1.at[0], rs1.at[0], right), remote(info_s, near.at[2], ss1.at[1], rs1.at[1], left)
    ]
    for copy in f_near:
        copy.start()
    f_line = [remote(fs.at[mine], fs.at[mine], ss2.at[j + 1], rs2.at[j + 1], line_peers[j]) for j in range(nz - 1)]
    for copy in f_line:
        copy.start()
    f_share = [remote(fs.at[behind(j)], fs.at[behind(j)], ss4.at[j], rs4.at[j], sibling) for j in range(nz)]
    f_share[0].start()

    halos = []
    for i, (src, dst, rows) in enumerate(((icev, iceh, 6), (ocean, och, 8), (sensv, sensh, 3))):
        halos.append(remote(src.at[pl.ds(ROWS_DEV - rows, rows)], dst.at[0], ss3.at[2 * i], rs3.at[2 * i], right))
        halos.append(remote(src.at[pl.ds(0, rows)], dst.at[1], ss3.at[2 * i + 1], rs3.at[2 * i + 1], left))
    up_now, down_now = p != PLANE - 1, p != 0

    def start_halos(up, down, which):
        @pl.when(up)
        def _():
            for i in which:
                halos[2 * i].start()

        @pl.when(down)
        def _():
            for i in which:
                halos[2 * i + 1].start()

    load_ice.wait()
    load_sens.wait()
    start_halos(up_now, down_now, (0, 1, 2))

    @pl.when(me == 0)
    def _():
        for ref in (iceh, sensh, och):
            ref[0] = jnp.zeros_like(ref[0])

    @pl.when(me == n - 1)
    def _():
        for ref in (iceh, sensh, och):
            ref[1] = jnp.zeros_like(ref[1])

    def wait_halos(which):
        @pl.when(me != n - 1)
        def _():
            for i in which:
                halos[2 * i].wait_send()
                halos[2 * i + 1].wait_recv()

        @pl.when(me != 0)
        def _():
            for i in which:
                halos[2 * i].wait_recv()
                halos[2 * i + 1].wait_send()

    tell = [remote(info_s, info.at[mine], ss1.at[2 + j], rs1.at[2 + j], line_peers[j]) for j in range(nz - 1)]
    tell += [remote(info_s, info.at[mine], ss1.at[nz + 2 + j], rs1.at[nz + 2 + j], cross_peers[j]) for j in range(nz)]
    info[mine] = info_s[...]

    keep_low = jnp.where(me == 0, 0.0, 1.0)
    keep_high = jnp.where(me == n - 1, 0.0, 1.0)
    rows = iota((128, 128), 0)
    diag = jnp.where(rows == iota((128, 128), 1), 1.0, 0.0)
    ones = jnp.ones((128, 128), bf16)
    not_first = rows > 0
    not_last = rows < 127

    def put(dst, pair, half, v):
        at = half * 384
        dst[pair, :, at : at + 128] = jnp.where(not_first, pltpu.roll(v, 1, 0), 0.0).astype(bf16)
        dst[pair, :, at + 128 : at + 256] = v.astype(bf16)
        dst[pair, :, at + 256 : at + 384] = jnp.where(not_last, pltpu.roll(v, 127, 0), 0.0).astype(bf16)

    def put_a(e, v):
        put(xa, e // 2, e % 2, v)

    def put_b(e, v):
        put(xb, (e - 1) // 2, (e - 1) % 2, v)

    def set_weights(layer):
        for s in range(2):
            at = (3 - 3 * s) * 384
            wall[layer, at : at + 384, s * 128 : s * 128 + 128] = jnp.zeros((384, 128), bf16)
        for a in range(3):
            for b in range(3):
                if layer < 3:
                    tile = cwv[layer * 9 + a * 3 + b]
                else:
                    tile = cwv[(layer - 3) * 9 + (2 - a) * 3 + 2 - b].T
                for s in range(2):
                    at = (a + s) * 384 + b * 128
                    wall[layer, at : at + 128, s * 128 : s * 128 + 128] = tile

    def spread(c, carry):
        e = 8 * c
        cells = oc[pl.ds(pl.multiple_of(e, 8), 8), :]
        wide = jnp.concatenate([(diag * cells[i : i + 1, :]).astype(bf16) for i in range(8)], axis=0)
        mask[pl.ds(e, 8)] = dot(wide, ones).reshape(8, 128, 128)
        return carry

    def stage(layer, src, q0, pairs, finish):
        odd = 0 if src is xa else 1
        lhs = src[pl.ds(q0, pairs)].reshape(pairs * 128, 768)
        rhs = src[pl.ds(q0 + 1, pairs)].reshape(pairs * 128, 768)
        acc = dot(jnp.concatenate([lhs, rhs], axis=1), wall[layer])
        for i in range(pairs):
            for s in range(2):
                finish(2 * (q0 + i) + odd + 1 + s, acc[i * 128 : i * 128 + 128, s * 128 : s * 128 + 128])

    def middle_a(e):
        return xa[e // 2, :, (e % 2) * 384 + 128 : (e % 2) * 384 + 256].astype(f32)

    def middle_b(e):
        return xb[(e - 1) // 2, :, ((e - 1) % 2) * 384 + 128 : ((e - 1) % 2) * 384 + 256].astype(f32)

    def sens_row(e):
        if e < 8:
            return sensh[0, e - 5].astype(f32)
        if e >= 40:
            return sensh[1, e - 40].astype(f32)
        return sensv[e - 8].astype(f32)

    def conv0(e, acc):
        t = jnp.tanh(acc + cb[0:1, :])
        m = mask[e]
        if 7 <= e <= 40:
            s0[e] = m * (1.0 - t * t)
        h1[e] = (middle_a(e) + m * t).astype(bf16)

    def conv1(e, acc):
        t = jnp.tanh(acc + cb[1:2, :])
        m = mask[e]
        if 6 <= e <= 41:
            s1[e] = m * (1.0 - t * t)
        put_a(e, middle_b(e) + m * t)

    def conv2(e, acc):
        t = jnp.tanh(acc + cb[2:3, :])
        m = mask[e]
        if 8 <= e < 40:
            img[e - 8] = (middle_a(e) + m * t).astype(bf16)
        put_b(e, sens_row(e) * (m * (1.0 - t * t)))

    def back2(e, acc):
        total = sens_row(e) + acc
        g[e] = total
        put_a(e, total * s1[e])

    def back1(e, acc):
        total = g[e] + acc
        g[e] = total
        put_b(e, total * s0[e])

    def back0(e, acc):
        sg[e - 8] = (g[e] + acc).astype(bf16)

    load_cw.wait()
    set_weights(0)
    oc[8:40, :] = ocean[...].astype(f32)
    lax.fori_loop(1, 5, spread, 0)

    def fill(q, carry):
        put(xa, q + 4, 0, icev[2 * q].astype(f32))
        put(xa, q + 4, 1, icev[2 * q + 1].astype(f32))
        return carry

    lax.fori_loop(0, ROWS_DEV // 2, fill, 0)
    for copy in f_near:
        copy.wait()
    lane, row = iota((3 * 128, 256), 1), iota((3 * 128, 256), 0)
    k, e = lane // 64, lax.rem(lane, 64)
    choose = jnp.where((e < E) & (row == (e + 24) // ROWS_DEV * 128 + k * ROWS_DEV + lax.rem(e + 24, ROWS_DEV)), 1.0, 0.0)
    own = jnp.concatenate([near[i] for i in range(3)], axis=1)
    ext_s[...] = dot(jnp.concatenate([own, jnp.zeros_like(own)], axis=0).astype(bf16), choose.astype(bf16))
    ext[0] = ext_s[...]
    f_ext = [remote(ext_s, ext.at[j + 1], ss9.at[j], rs9.at[j], plane_peers[j]) for j in range(3)]
    for copy in f_ext:
        copy.start()
    for copy in tell:
        copy.start()
    def inner0(c, carry):
        q0 = 4 + 5 * c
        lhs = xa[pl.ds(q0, 5)].reshape(5 * 128, 768)
        rhs = xa[pl.ds(q0 + 1, 5)].reshape(5 * 128, 768)
        acc = dot(jnp.concatenate([lhs, rhs], axis=1), wall[0])
        for i in range(5):
            for s in range(2):
                e = 2 * (q0 + i) + 1 + s
                t = jnp.tanh(acc[i * 128 : i * 128 + 128, s * 128 : s * 128 + 128] + cb[0:1, :])
                m = mask[e]
                s0[e] = m * (1.0 - t * t)
                at = (1 - s) * 384 + 128
                h1[e] = (xa[q0 + i + s, :, at : at + 128].astype(f32) + m * t).astype(bf16)
        return carry

    start_halos((p == PLANE - 1) & (me != n - 1), (p == 0) & (me != 0), (0, 1))
    lax.fori_loop(0, 3, inner0, 0)
    for layer in range(1, 6):
        set_weights(layer)
    l16[...] = jnp.zeros_like(l16)
    l16[0:F, :] = lift[...].astype(f32)
    lift16 = l16[...].astype(bf16)
    eight = jnp.concatenate([lift16] * 8, axis=0)
    of_row = iota((128, 128), 0) // FP
    for i in range(8):
        bd[:, i * 128 : i * 128 + 128] = jnp.where(of_row == i, eight, jnp.zeros_like(eight))
    cm = col_map[...].astype(bf16)

    def record(rec):
        owner, loc = rec[0:1, :].astype(jnp.int32), rec[1:2, :].astype(jnp.int32)
        return lax.div(owner, PLANE), lax.div(lax.rem(owner, PLANE), 2), lax.rem(owner, 2), loc, rec[2:3, :]

    for copy in f_ext:
        copy.wait()
    nf = 2 * nz * OWN
    spots = lax.rem(iota((E, 256), 1), 64) == iota((E, 256), 0)
    spots = jnp.where(spots, 1.0, 0.0).astype(bf16)
    for j in range(4):
        oz, ochip, ocore, loc, w = record(ext[(4 - j) % 4])
        at = jnp.where(ochip == chip, (ocore * nz + oz) * OWN + loc, -1)
        one = jnp.where(iota((nf, 256), 0) == at, w, 0.0).astype(bf16)
        wsum[j * E : j * E + E, :] = dot(spots, one, 1, 1).astype(bf16)

    for j in range(1, nz):
        f_line[j - 1].wait()
        f_share[j].start()

    def plane(src, dst, at, size, send, recv, first):
        return [
            remote(
                src.at[j, pl.ds(at, size)], dst.at[j, pl.ds(at, size)], send.at[first + j], recv.at[first + j],
                plane_peers[j - 1],
            )
            for j in range(1, 4)
        ]

    for copy in f_share:
        copy.wait()
    ps[...] = dot(wsum[...], fs[...].reshape(nf, WIDE)).astype(bf16).reshape(4, E, WIDE)
    f_plane = [plane(ps, pv, 16 * c, 16, ss5, rs5, 4 * c) for c in range(3)]
    for copy in f_plane[0]:
        copy.start()
    for copy in tell:
        copy.wait()

    row, lane = iota((64, 128), 0), iota((64, 128), 1)
    same = lax.rem(lane, ROWS_DEV) == row // 16 * 8 + lax.rem(row, 8)
    low = lax.rem(row, 16) < 8
    pick_low = jnp.where(same & low, 1.0, 0.0).astype(bf16)
    pick_high = jnp.where(same & ~low, 1.0, 0.0).astype(bf16)
    for c in range(2 * nz):
        oz, ochip, ocore, loc, w = record(info[c])
        at = jnp.where((oz == z) & (ocore == core), lax.rem(ochip + 4 - chip, 4) * OWN + loc, -1)
        one = jnp.where(iota((4 * OWN, 128), 0) == at, w, 0.0).astype(bf16)
        for half, pick in enumerate((pick_low, pick_high)):
            part = dot(pick, one, 1, 1).astype(bf16)
            for i in range(4):
                to = (i * 2 * nz + c) * 16
                vt[to : to + 16, half * 128 : half * 128 + 128] = part[i * 16 : i * 16 + 16]
    for copy in f_plane[1]:
        copy.start()
    wait_halos((0, 1))
    oc[0:8, :] = och[0].astype(f32) * keep_low
    oc[40:48, :] = och[1].astype(f32) * keep_high
    spread(0, 0)
    spread(5, 0)
    for i in range(6):
        put_a(2 + i, iceh[0, i].astype(f32) * keep_low)
        put_a(40 + i, iceh[1, i].astype(f32) * keep_high)
    stage(0, xa, 1, 3, conv0)
    stage(0, xa, 19, 3, conv0)
    start_halos((p == PLANE - 1) & (me != n - 1), (p == 0) & (me != 0), (2,))
    icr[...] = jnp.zeros_like(icr)

    def arrive(c):
        for copy in f_plane[c]:
            copy.wait()
        if c == 0:
            for copy in f_plane[2]:
                copy.start()
        x = jnp.concatenate([
            sum((pv if j else ps)[j, 16 * c : 16 * c + 16, i * 128 : i * 128 + 128].astype(f32) for j in range(4)) for i in range(F)
        ], axis=0)
        erow = iota((16, 1), 0) + 16 * c
        inside = jnp.where(erow < 8, keep_low, jnp.where(erow < 40, 1.0, keep_high))
        y = dot(x.astype(bf16), cm)
        for i in range(F):
            icr[16 * c : 16 * c + 16, i, :] = y[16 * i : 16 * i + 16] * inside

    def lift_eight(c):
        wide = dot(icr[8 * c : 8 * c + 8].reshape(8 * FP, 128).astype(bf16), bd[...], 0, 0)
        for i in range(8):
            e = 8 * c + i
            if 3 <= e <= 44:
                put_b(e, h1[e].astype(f32) + wide[:, i * 128 : i * 128 + 128])

    def t_line(c):
        return [
            remote(prg.at[c, mine], prg.at[c, mine], ss6.at[c * nz + j], rs6.at[c * nz + j], lax.rem(z + j, nz) * PLANE + p)
            for j in range(1, nz)
        ]

    def t_share(c):
        part = prg.at[c, pl.ds(core * nz, nz)]
        return remote(part, part, ss7.at[c], rs7.at[c], sibling)

    lines, shares = [], []

    def project(c):
        wide = jnp.concatenate([g[8 * c + 8 + i].astype(bf16) for i in range(8)], axis=1)
        y = dot(dot(bd[...], wide, 1, 1).astype(bf16), cm, 1, 1)
        fg[...] = y.reshape(8, FP, 128)
        for half in range(2):
            for i in range(5):
                f3[half * 8 : half * 8 + 8, i * 128 : i * 128 + 128] = fg[:, half * 5 + i, :]
        prg[c, mine] = f3[...].astype(bf16)
        lines.append(t_line(c))
        for copy in lines[c]:
            copy.start()

    def relay(c):
        for copy in lines[c]:
            copy.wait()
        shares.append(t_share(c))
        shares[c].start()

    layers = {1: (1, xb, 1, conv1), 2: (2, xa, 2, conv2), 3: (5, xb, 2, back2), 4: (4, xa, 3, back1), 5: (3, xb, 3, back0)}

    def sens_ready():
        wait_halos((2,))

    def back0_loop(first, count):
        def body(i, carry):
            stage(3, xb, 3 + first + STEP * i, STEP, back0)
            return carry

        lax.fori_loop(0, count, body, 0)

    events = {"back0": back0_loop, "arrive": arrive, "lift": lift_eight, "sens": sens_ready, "project": project, "relay": relay}
    for name, *rest in PLAN:
        if name == "conv":
            which, k0, count = rest
            layer, src, q, finish = layers[which]
            stage(layer, src, k0 + q, count, finish)
        else:
            events[name](*rest)
    for copy in shares:
        copy.wait()
    total = dot(vt[...], prg[...].reshape(2 * nf, HALF), 0, 0).astype(bf16)
    ts[:, 0:OWN, :] = total[0 : 4 * OWN].reshape(4, OWN, HALF)
    ts[:, OWN : 2 * OWN, :] = total[4 * OWN : 8 * OWN].reshape(4, OWN, HALF)
    t_plane = plane(ts, tr, 0, 2 * OWN, ss8, rs8, 0)
    for copy in t_plane:
        copy.start()
    for copy in t_plane:
        copy.wait()
    for half in range(2):
        for i in range(5):
            x = sum((tr if j else ts)[j, half * OWN : half * OWN + OWN, i * 128 : i * 128 + 128].astype(f32) for j in range(4))
            for q in range(grad.shape[0]):
                grad[q, half * 5 + i] = x[q * 8 : q * 8 + 8]


def deliver_kernel(img, sg, grad, img_out, sg_out, grad_out, sems):
    copies = [
        pltpu.make_async_copy(src, dst, sems.at[i])
        for i, (src, dst) in enumerate(((img, img_out), (sg, sg_out), (grad, grad_out)))
    ]
    for copy in copies:
        copy.start()
    for copy in copies:
        copy.wait()


def body(
    forcing, ice_state, sensitivity, owner_device, panel_slot, row_offset,
    intersection_weight, col_map, ocean_mask, lift_weight, conv_weight, conv_bias,
):
    n = lax.axis_size("tile")
    nz = n // PLANE
    nf = 2 * nz * OWN
    V, D = pltpu.VMEM, pltpu.SemaphoreType.DMA
    vmem, hbm = pl.BlockSpec(memory_space=pltpu.VMEM), pl.BlockSpec(memory_space=pl.ANY)
    panels, pr = forcing.shape[:2]
    field = (E, 128, 128)
    tile = (ROWS_DEV, 128, 128)
    shapes = [
        jax.ShapeDtypeStruct(tile, bf16),
        jax.ShapeDtypeStruct(tile, bf16),
        jax.ShapeDtypeStruct((panels, F, pr, 128), f32),
    ]
    results = pl.pallas_call(
        functools.partial(program_kernel, n),
        out_shape=[pltpu.VMEM(x.shape, x.dtype) for x in shapes],
        in_specs=[hbm] * 12,
        out_specs=[vmem, vmem, vmem],
        scratch_shapes=[
            V((4, 128), f32), V((2 * nz, 4, 128), f32), V((3, 4, 128), f32), V((8, 256), f32), V((4, 8, 256), f32),
            V((OWN, WIDE), f32), V((16, HALF), f32),
            V((2 * nz, OWN, WIDE), bf16), V((4 * E, nf), bf16),
            V((4, E, WIDE), bf16), V((4, E, WIDE), bf16), V((4, 2 * nz, 16, HALF), bf16), V((2 * nf, 256), bf16),
            V((4, 2 * OWN, HALF), bf16), V((4, 2 * OWN, HALF), bf16), V((FP, 128), f32),
            V((2, 6, 128, 128), bf16), V((2, 3, 128, 128), bf16), V((2, 8, 128), jnp.int32),
            V((E // 2, 128, 768), bf16), V((E // 2, 128, 768), bf16), V(field, f32), V(field, f32),
            V(field, f32), V(field, f32), V(field, bf16),
            V((6, 1536, 256), bf16), V((E, 128), f32), V((E, FP, 128), f32), V((8, FP, 128), f32),
            V(tile, bf16), V(tile, bf16), V((27, 128, 128), bf16), V((128, 1024), bf16),
            D((2 * nz + 2,)), D((2 * nz + 2,)), D((nz,)), D((nz,)), D((6,)), D((6,)), D((nz,)), D((nz,)), D((12,)), D((12,)),
            D((4 * nz,)), D((4 * nz,)), D((4,)), D((4,)), D((4,)), D((4,)), D((3,)), D((3,)), D((12,)),
            V((ROWS_DEV, 128), jnp.int32), V((K, ROWS_DEV), jnp.int32), V((K, ROWS_DEV), jnp.int32), V((K, ROWS_DEV), jnp.int32),
            V((K, ROWS_DEV), f32), V((panels, F, pr, 128), bf16), V((128, 128), f32), V((F, 128), bf16), V((3, 128), f32),
        ],
        compiler_params=pltpu.CompilerParams(
            vmem_limit_bytes=56 * 1024 * 1024, collective_id=1, has_side_effects=True
        ),
    )(ice_state, sensitivity, ocean_mask, owner_device.T, panel_slot.T, row_offset.T, intersection_weight.T,
      forcing.transpose(0, 2, 1, 3), col_map, lift_weight, conv_weight.reshape(27, 128, 128), conv_bias)
    img, sg, grad = pl.pallas_call(
        deliver_kernel,
        out_shape=shapes,
        in_specs=[vmem, vmem, vmem],
        out_specs=[hbm, hbm, hbm],
        scratch_shapes=[D((3,))],
    )(*[pltpu.with_memory_space_constraint(x, pltpu.VMEM) for x in results])
    return img, sg, grad.transpose(0, 2, 1, 3)


def solution(mesh):
    in_specs = (
        P(("member", "tile"), None, None, None),
        P(("member", "tile"), None, None),
        P(("member", "tile"), None, None),
        P("tile", None),
        P("tile", None),
        P("tile", None),
        P("tile", None),
        P(),
        P("tile", None),
        P(),
        P(),
        P(),
    )
    out_specs = (
        P(("member", "tile"), None, None),
        P(("member", "tile"), None, None),
        P(("member", "tile"), None, None, None),
    )
    return jax.shard_map(body, mesh=mesh, in_specs=in_specs, out_specs=out_specs, check_vma=False)
```
